32 devices in a mesh: head: 2 (over core), seq: 16 (over z, y, x).
Axes of the slice: x: 2, y: 2, z: 4, core: 2. Of those that a mesh axis runs over, the one named last changes fastest.
Arguments:
- tokens: bfloat16 [6144, 4096], P('seq', 'head'), may hold values from -6 to 6
- w_qkv: bfloat16 [4096, 12288], P('seq', 'head'), may hold values from -0.09375 to 0.09375
- conv_w: float32 [4, 12288], P(None, 'head'), may hold values from -3 to 3
- prev_tail: bfloat16 [3, 12288], P(None, 'head'), may hold values from -6 to 6
- w_one: bfloat16 [16, 256, 1024], P('head'), may hold values from -0.375 to 0.375
- w_three: bfloat16 [16, 256, 1024], P('head'), may hold values from -0.375 to 0.375
- w_two: bfloat16 [16, 256, 1024], P('head'), may hold values from -0.1875 to 0.1875
- out_gain: float32 [4096], P('head'), may hold values from 0.5 to 1.5
Outputs:
- layer_out: float32 [6144, 4096], P('seq', 'head')
The draws below stay inside these ranges and needn't reach their ends.
All inputs are finite; a program needn't handle non-finite values.
Results may differ from the reference program's by a relative error of at most 0.018.
Values may be sent and summed in bfloat16 or wider, within the bound.
No kernel may reach another device: no remote copies, remote signals or barrier semaphores. Data moves between devices by JAX's collectives and lax.ppermute only.
A program may use at most 192 MiB of HBM per device.

```python
import jax
import jax.numpy as jnp
from jax import lax

D = 4096
HEADS = 16
DH = 256
FW = 1024
NS_STEPS = 3
TOKENS = 6144


def shard_levels(rng, extent, split, least, high):
    def one(position, blocks):
        heights = jax.random.uniform(jax.random.fold_in(jax.random.fold_in(rng, 6), position), (blocks,), jnp.float32, least / len(split), high / len(split))
        return jnp.repeat(jnp.exp(heights), extent[position] // blocks).reshape((-1,) + (1,) * (len(extent) - position - 1))

    loudness = one(*split[0])
    for cut in split[1:]:
        loudness = loudness * one(*cut)
    return loudness


def noise(stream_key, extent, deviation, reach, pieces=(), kind=jnp.bfloat16):
    level = shard_levels(stream_key, extent, pieces, -0.22, 0.18) if pieces else 1.0
    array = jax.random.normal(stream_key, extent, jnp.float32) * deviation * level
    return jnp.minimum(jnp.maximum(array, -reach), reach).astype(kind)


def setup_inputs(seed: int = 0) -> dict:
    keys = jax.random.split(jax.random.key(seed), 9)
    return {
        "tokens": noise(keys[0], (TOKENS, D), 1.0, 6.0, ((0, 16), (1, 2))),
        "w_qkv": noise(keys[1], (D, 3 * D), D ** -0.5, 0.09375, ((0, 16), (1, 2))),
        "conv_w": noise(keys[2], (4, 3 * D), 0.5, 3.0, ((1, 2),), jnp.float32),
        "prev_tail": noise(keys[3], (3, 3 * D), 1.0, 6.0, ((1, 2),)),
        "w_one": noise(keys[4], (HEADS, DH, FW), DH ** -0.5, 0.375, ((0, 2),)),
        "w_three": noise(keys[5], (HEADS, DH, FW), DH ** -0.5, 0.375, ((0, 2),)),
        "w_two": noise(keys[6], (HEADS, DH, FW), FW ** -0.5, 0.1875, ((0, 2),)),
        "out_gain": jnp.clip(0.5 + 1.0 * jax.random.uniform(keys[7], (D,), jnp.float32) ** shard_levels(keys[7], (D,), ((0, 2),), -0.2, 0.2), 0.5, 1.5),
    }


coef_a = 3.4445
coef_b = -4.775
coef_c = 2.0315

def conv_mix(padded, conv_w, count):
    total = jnp.zeros((count, padded.shape[1]), jnp.float32)
    for shift_back in range(4):
        start = 3 - shift_back
        total = total + conv_w[shift_back][None, :] * padded[start:start + count].astype(jnp.float32)
    return total

def rms_silu(part):
    act = part * jax.nn.sigmoid(part)
    return (act * lax.rsqrt(lax.optimization_barrier(jnp.mean(act * act, axis=-1, keepdims=True)) + 1e-06)).astype(jnp.bfloat16)

def fdot(left, right):
    return jnp.dot(left.astype(jnp.float32), right.astype(jnp.float32), precision=lax.Precision.HIGHEST)

def orthogonalize(grad):
    norm = jnp.sqrt(jnp.sum(grad * grad)) + 1e-07
    ortho = (grad / norm).astype(jnp.bfloat16)
    for step in range(NS_STEPS):
        gram = fdot(ortho, ortho.T).astype(jnp.bfloat16)
        square = fdot(gram, gram)
        blend = (coef_b * gram.astype(jnp.float32) + coef_c * square).astype(jnp.bfloat16)
        ortho = (coef_a * ortho.astype(jnp.float32) + fdot(blend, ortho)).astype(jnp.bfloat16)
    return ortho

def one_head(query, key, value, one, three, two, gain):
    h_one = jnp.dot(key, one, preferred_element_type=jnp.float32)
    h_three = jnp.dot(key, three, preferred_element_type=jnp.float32)
    sig = jax.nn.sigmoid(h_one)
    act = (h_one * sig * h_three).astype(jnp.bfloat16)
    back = jnp.dot(value, two, preferred_element_type=jnp.float32)
    d_one = (back * h_three * sig * (1.0 + h_one * (1.0 - sig))).astype(jnp.bfloat16)
    d_three = (back * h_one * sig).astype(jnp.bfloat16)
    g_one = fdot(key.T, d_one)
    g_three = fdot(key.T, d_three)
    g_two = fdot(value.T, act)
    new_one = (one.astype(jnp.float32) + orthogonalize(g_one).astype(jnp.float32)).astype(jnp.bfloat16)
    new_three = (three.astype(jnp.float32) + orthogonalize(g_three).astype(jnp.float32)).astype(jnp.bfloat16)
    new_two = (two.astype(jnp.float32) + orthogonalize(g_two).astype(jnp.float32)).astype(jnp.bfloat16)
    q_one = jnp.dot(query, new_one, preferred_element_type=jnp.float32)
    q_three = jnp.dot(query, new_three, preferred_element_type=jnp.float32)
    q_act = (q_one * jax.nn.sigmoid(q_one) * q_three).astype(jnp.bfloat16)
    fast_out = jnp.dot(q_act, new_two.T, preferred_element_type=jnp.float32)
    normed = fast_out * lax.rsqrt(lax.optimization_barrier(jnp.mean(fast_out * fast_out, axis=-1, keepdims=True)) + 1e-05)
    return (normed * gain[None, :]).astype(jnp.float32)

def reference(tokens, w_qkv, conv_w, prev_tail, w_one, w_three, w_two, out_gain):
    projected = jnp.dot(tokens, w_qkv, preferred_element_type=jnp.float32).astype(jnp.bfloat16)
    padded = jnp.concatenate([prev_tail, projected], axis=0)
    mixed = conv_mix(padded, conv_w, TOKENS)
    mixed = mixed.reshape(TOKENS, HEADS, 3, DH)
    outputs = []
    for head_no in range(HEADS):
        query = rms_silu(mixed[:, head_no, 0])
        key = rms_silu(mixed[:, head_no, 1])
        value = mixed[:, head_no, 2].astype(jnp.bfloat16)
        gain = out_gain[head_no * DH:(head_no + 1) * DH]
        outputs.append(one_head(query, key, value, w_one[head_no], w_three[head_no], w_two[head_no], gain))
    return jnp.concatenate(outputs, axis=1)
```

```python
import functools

import jax
import jax.numpy as jnp
from jax import lax
from jax.experimental import pallas as pl
from jax.experimental.pallas import tpu as pltpu
from jax.sharding import PartitionSpec as P

NS_STEPS = 3


coef_a = 3.4445
coef_b = -4.775
coef_c = 2.0315


def shifted(value, axis, steps):
    count = lax.axis_size(axis)
    leading, last = (max(0, -steps), min(count, count - steps))
    return lax.ppermute(value, axis, [(source, source + steps) for source in range(leading, last)])


def conv_mix(padded, conv_w, count):
    total = jnp.zeros((count, padded.shape[1]), jnp.float32)
    for shift_back in range(4):
        start = 3 - shift_back
        total = total + conv_w[shift_back][None, :] * padded[start : start + count].astype(
            jnp.float32
        )
    return total


def rms_silu(part):
    act = part * jax.nn.sigmoid(part)
    return (act * lax.rsqrt(jnp.mean(act * act, axis=-1, keepdims=True) + 1e-06)).astype(
        jnp.bfloat16
    )


def orthogonalize(grad, total_fn, gram_fn):
    squares = total_fn(jnp.sum(grad * grad, axis=(1, 2)))
    norm = jnp.sqrt(squares)[:, None, None] + 1e-07
    ortho = (grad / norm).astype(jnp.bfloat16)
    for step in range(NS_STEPS):
        partial_gram = jnp.einsum("mik,mjk->mij", ortho, ortho, preferred_element_type=jnp.float32)
        gram = gram_fn(partial_gram).astype(jnp.bfloat16)
        square = jnp.einsum("mik,mkj->mij", gram, gram, preferred_element_type=jnp.float32)
        blend = (coef_b * gram.astype(jnp.float32) + coef_c * square).astype(jnp.bfloat16)
        moved = jnp.einsum("mik,mkj->mij", blend, ortho, preferred_element_type=jnp.float32)
        ortho = (coef_a * ortho.astype(jnp.float32) + moved).astype(jnp.bfloat16)
    return ortho


def plain_device(tokens, w_qkv, conv_w, prev_tail, w_one, w_three, w_two, out_gain):
    whole = lax.all_gather(tokens, "head", axis=1, tiled=True)
    rows = whole.shape[0]
    heads_here = w_one.shape[0]
    head_dim = w_one.shape[1]
    projected = jnp.dot(
        whole, lax.all_gather(w_qkv, "seq", axis=0, tiled=True), preferred_element_type=jnp.float32
    ).astype(jnp.bfloat16)
    arrived = shifted(projected[rows - 3 :], "seq", 1)
    before = jnp.where(lax.axis_index("seq") == 0, prev_tail, arrived)
    mixed = conv_mix(jnp.concatenate([before, projected], axis=0), conv_w, rows)
    mixed = mixed.reshape(rows, heads_here, 3, head_dim)
    query = rms_silu(mixed[:, :, 0])
    key = rms_silu(mixed[:, :, 1])
    value = mixed[:, :, 2].astype(jnp.bfloat16)
    h_one = jnp.einsum("the,hef->thf", key, w_one, preferred_element_type=jnp.float32)
    h_three = jnp.einsum("the,hef->thf", key, w_three, preferred_element_type=jnp.float32)
    sig = jax.nn.sigmoid(h_one)
    act = (h_one * sig * h_three).astype(jnp.bfloat16)
    back = jnp.einsum("the,hef->thf", value, w_two, preferred_element_type=jnp.float32)
    d_one = (back * h_three * sig * (1.0 + h_one * (1.0 - sig))).astype(jnp.bfloat16)
    d_three = (back * h_one * sig).astype(jnp.bfloat16)
    g_one = jnp.einsum("the,thf->hef", key, d_one, preferred_element_type=jnp.float32)
    g_three = jnp.einsum("the,thf->hef", key, d_three, preferred_element_type=jnp.float32)
    g_two = jnp.einsum("the,thf->hef", value, act, preferred_element_type=jnp.float32)
    grads = jnp.concatenate([g_one, g_three, g_two], axis=0)
    summed = lax.psum(grads, "seq")
    ortho = orthogonalize(summed, lambda value_in: value_in, lambda value_in: value_in)
    stacked = jnp.concatenate([w_one, w_three, w_two], axis=0)
    renewed = (stacked.astype(jnp.float32) + ortho.astype(jnp.float32)).astype(jnp.bfloat16)
    new_one = renewed[:heads_here]
    new_three = renewed[heads_here : 2 * heads_here]
    new_two = renewed[2 * heads_here :]
    q_one = jnp.einsum("the,hef->thf", query, new_one, preferred_element_type=jnp.float32)
    q_three = jnp.einsum("the,hef->thf", query, new_three, preferred_element_type=jnp.float32)
    q_act = (q_one * jax.nn.sigmoid(q_one) * q_three).astype(jnp.bfloat16)
    fast_out = jnp.einsum("thf,hef->the", q_act, new_two, preferred_element_type=jnp.float32)
    normed = fast_out * lax.rsqrt(jnp.mean(fast_out * fast_out, axis=-1, keepdims=True) + 1e-05)
    normed = normed * out_gain.reshape(heads_here, head_dim)[None, :, :]
    return normed.reshape(rows, heads_here * head_dim)


HALO = 8
FIRST_HALF_BIT = 8
PARTNER_BIT = 4
PLANE = (0, 1, 2, 3)


def flip(value, bits):
    count = lax.axis_size("seq")
    return lax.ppermute(value, "seq", [(source, source ^ bits) for source in range(count)])


def other_core(value):
    return lax.ppermute(value, "head", [(0, 1), (1, 0)])


def after(value, done):
    return lax.optimization_barrier((value, done))[0]


def whole_call(kernel, out_shape, scratch=(), aliases=None, scalars=1, inputs=0, name=None):
    vmem = pl.BlockSpec(memory_space=pltpu.VMEM)
    smem = pl.BlockSpec(memory_space=pltpu.SMEM)
    many = isinstance(out_shape, (list, tuple))
    return pl.pallas_call(
        kernel,
        out_shape=out_shape,
        in_specs=[smem] * scalars + [vmem] * inputs,
        out_specs=[vmem] * len(out_shape) if many else vmem,
        scratch_shapes=list(scratch),
        input_output_aliases=aliases or {},
        name=name,
    )


def dot(left, right, dims=((1,), (0,))):
    return lax.dot_general(left, right, (dims, ((), ())), preferred_element_type=jnp.float32)


def project_mix(near, far, weight_ref, conv_ref, tail_ref, first, line_ref, half):
    total = dot(near, weight_ref[:half]) + dot(far, weight_ref[half:])
    line_ref[...] = total.astype(jnp.bfloat16).astype(jnp.float32)
    line_ref[:HALO] = jnp.where(first != 0, tail_ref[...], line_ref[:HALO])
    rows = line_ref.shape[0] - HALO
    mixed = conv_ref[0:1] * line_ref[pl.ds(HALO, rows), :]
    for back in range(1, 4):
        mixed = mixed + conv_ref[back : back + 1] * line_ref[pl.ds(HALO - back, rows), :]
    return mixed


def grads_kernel(blocks, started, *refs):
    first_ref = refs[0]
    tokens = refs[1 : 1 + 2 * blocks]
    weight, conv, tail, one, three, two = refs[1 + 2 * blocks : 7 + 2 * blocks]
    rest = refs[7 + 2 * blocks :]
    before = None
    if started:
        before, rest = rest[0], rest[1:]
    out, line, keys, values, acts, d_ones, d_threes = rest
    half = weight.shape[0] // 2
    dim = one.shape[0]
    chunk = line.shape[0]
    rows = chunk - HALO
    place = 0
    for block in range(blocks):
        near, far = tokens[2 * block], tokens[2 * block + 1]
        for part in range(near.shape[0] // chunk):
            span = slice(part * chunk, (part + 1) * chunk)
            where = slice(place * rows, (place + 1) * rows)
            mixed = project_mix(
                near[span], far[span], weight, conv, tail, first_ref[place], line, half
            )
            key = rms_silu(mixed[:, :dim])
            value = mixed[:, dim:].astype(jnp.bfloat16)
            h_one = dot(key, one[...])
            h_three = dot(key, three[...])
            back = dot(value, two[...])
            sig = jax.nn.sigmoid(h_one)
            gate = h_one * sig
            keys[where] = key
            values[where] = value
            acts[where] = (gate * h_three).astype(jnp.bfloat16)
            d_ones[where] = (back * h_three * sig * (1.0 + h_one * (1.0 - sig))).astype(
                jnp.bfloat16
            )
            d_threes[where] = (back * gate).astype(jnp.bfloat16)
            place += 1
    pairs = ((keys, d_ones), (keys, d_threes), (values, acts))
    for index, (left, right) in enumerate(pairs):
        grad = dot(left[...], right[...], ((0,), (0,)))
        if before is not None:
            grad = grad + before[index]
        out[index] = grad


def query_kernel(blocks, *refs):
    first_ref = refs[0]
    tokens = refs[1 : 1 + 2 * blocks]
    weight, conv, tail = refs[1 + 2 * blocks : 4 + 2 * blocks]
    out, line = refs[4 + 2 * blocks :]
    half = weight.shape[0] // 2
    chunk = line.shape[0]
    rows = chunk - HALO
    place = 0
    for block in range(blocks):
        near, far = tokens[2 * block], tokens[2 * block + 1]
        for part in range(near.shape[0] // chunk):
            span = slice(part * chunk, (part + 1) * chunk)
            mixed = project_mix(
                near[span], far[span], weight, conv, tail, first_ref[place], line, half
            )
            out[place * rows : (place + 1) * rows] = rms_silu(mixed)
            place += 1


def renew_kernel(mine, sent, one, three, two, out):
    orthos = []
    for index in range(3):
        grad = mine[index] + sent[index].astype(jnp.float32)
        norm = jnp.sqrt(jnp.sum(grad * grad, keepdims=True)) + 1e-07
        orthos.append((grad / norm).astype(jnp.bfloat16))
    for step in range(NS_STEPS):
        grams = [dot(v, v, ((1,), (1,))).astype(jnp.bfloat16) for v in orthos]
        squares = [dot(v, v) for v in grams]
        blends = [
            (coef_b * g.astype(jnp.float32) + coef_c * q).astype(jnp.bfloat16)
            for g, q in zip(grams, squares)
        ]
        orthos = [
            (coef_a * v.astype(jnp.float32) + dot(m, v)).astype(jnp.bfloat16)
            for v, m in zip(orthos, blends)
        ]
    for index, old in enumerate((one, three, two)):
        fresh = old[...].astype(jnp.float32) + orthos[index].astype(jnp.float32)
        out[index] = fresh.astype(jnp.bfloat16)


def answer_kernel(query, fresh, gain, out):
    q_one = dot(query[...], fresh[0])
    q_three = dot(query[...], fresh[1])
    q_act = (q_one * jax.nn.sigmoid(q_one) * q_three).astype(jnp.bfloat16)
    fast_out = dot(q_act, fresh[2], ((1,), (1,)))
    scale = lax.rsqrt(jnp.mean(fast_out * fast_out, axis=-1, keepdims=True) + 1e-05)
    out[...] = (fast_out * scale * gain[...]).astype(jnp.bfloat16)


def spread_weights(part, seat, core, ready=None):
    depth, heads, width = part.shape
    quad = len(PLANE)
    high = seat // FIRST_HALF_BIT
    low = (seat // PARTNER_BIT) % 2
    spot = seat % quad
    flat = part.reshape(depth, heads * width)
    if ready is not None:
        flat = after(flat, ready)
    kept = lax.dynamic_slice(flat, (0, high * quad * width), (depth, quad * width))
    given = lax.dynamic_slice(flat, (0, (1 - high) * quad * width), (depth, quad * width))
    crossed = flip(given, FIRST_HALF_BIT)
    groups = []
    for source in (kept, crossed):
        group = jnp.zeros((quad * depth, width), part.dtype)
        for bits in PLANE:
            piece = lax.dynamic_slice(source, (0, (spot ^ bits) * width), (depth, width))
            if bits:
                piece = flip(piece, bits)
            group = lax.dynamic_update_slice(group, piece, ((spot ^ bits) * depth, 0))
        groups.append(group)
    size = quad * depth
    weight = jnp.zeros((4 * size, width), part.dtype)
    for index, group in enumerate(groups):
        side = (high ^ index) ^ core
        weight = lax.dynamic_update_slice(weight, group, ((side * 2 + low) * size, 0))
        partner = flip(group, PARTNER_BIT)
        weight = lax.dynamic_update_slice(weight, partner, ((side * 2 + 1 - low) * size, 0))
    return weight, crossed


def head_device(tokens, w_qkv, conv_w, prev_tail, w_one, w_three, w_two, out_gain):
    count = lax.axis_size("seq")
    seat = lax.axis_index("seq")
    core = lax.axis_index("head")
    heads, dim, hidden = w_one.shape
    rows = tokens.shape[0]
    wide = 3 * dim
    quad = len(PLANE)
    head_of = lambda place: (place // FIRST_HALF_BIT) * quad + place % quad
    head = head_of(seat)

    columns = w_qkv.reshape(w_qkv.shape[0], heads, wide)
    weight_kv, crossed = spread_weights(columns[:, :, dim:], seat, core)

    half = rows // 2
    before = shifted(tokens[rows - HALO :], "seq", 1)
    upper = jnp.concatenate([before, tokens[:half]], axis=0)
    lower = tokens[half - HALO :]
    pair = jnp.concatenate([upper, lower], axis=0)
    chunk = half + HALO

    near = {0: [pair]}
    near[1] = [flip(pair, 1)]
    near[2] = [flip(pair, 2)]
    near[3] = [flip(near[1][0], 2)]
    far_bit = FIRST_HALF_BIT
    held = [after(upper, crossed), lower]
    held[1] = after(lower, crossed)
    near[far_bit] = [flip(v, far_bit) for v in held]
    near[far_bit | 1] = [flip(v, 1) for v in near[far_bit]]
    near[far_bit | 2] = [flip(v, 2) for v in near[far_bit]]
    near[far_bit | 3] = [flip(v, 1) for v in near[far_bit | 2]]
    far = {bits: [other_core(v) for v in values] for bits, values in near.items()}
    weight_q, _ = spread_weights(columns[:, :, :dim], seat, core, near[far_bit][1])

    own_conv = lax.dynamic_slice(conv_w, (0, head * wide), (4, wide))
    own_tail = lax.dynamic_slice(prev_tail, (0, head * wide), (3, wide)).astype(jnp.float32)
    own_tail = jnp.pad(own_tail, ((HALO - 3, 0), (0, 0)))
    pick = lambda value: lax.dynamic_index_in_dim(value, head, 0, keepdims=False)
    one, three, two = pick(w_one), pick(w_three), pick(w_two)
    gain = lax.dynamic_slice(out_gain, (head * dim,), (dim,)).reshape(1, dim)

    def operands(bits):
        flat = []
        for left, right in zip(near[bits], far[bits]):
            flat += [left, right]
        first = jnp.stack([(seat == bits).astype(jnp.int32), jnp.int32(0)])
        return len(near[bits]), first, flat

    order = [0, 1, 2, 3] + [far_bit | bits for bits in PLANE]
    grads = None
    lines = pltpu.VMEM((chunk, 2 * dim), jnp.float32)
    wide_scratch = lambda n: pltpu.VMEM((rows, n), jnp.bfloat16)
    for bits in order:
        blocks, first, flat = operands(bits)
        args = [first, *flat, weight_kv, own_conv[:, dim:], own_tail[:, dim:], one, three, two]
        started = grads is not None
        if started:
            args.append(grads)
        grads = whole_call(
            functools.partial(grads_kernel, blocks, started),
            jax.ShapeDtypeStruct((3, dim, hidden), jnp.float32),
            scratch=[lines, wide_scratch(dim), wide_scratch(dim)] + [wide_scratch(hidden)] * 3,
            aliases={len(args) - 1: 0} if started else None,
            inputs=len(args) - 1,
            name="grads_%d" % bits,
        )(*args)

    sent = flip(grads.astype(jnp.bfloat16), PARTNER_BIT)

    queries = {}
    for bits in order:
        blocks, first, flat = operands(bits)
        args = [first, *flat, weight_q, own_conv[:, :dim], own_tail[:, :dim]]
        queries[bits] = whole_call(
            functools.partial(query_kernel, blocks),
            jax.ShapeDtypeStruct((rows, dim), jnp.bfloat16),
            scratch=[pltpu.VMEM((chunk, dim), jnp.float32)],
            inputs=len(args) - 1,
            name="query_%d" % bits,
        )(*args)

    fresh = whole_call(
        renew_kernel,
        jax.ShapeDtypeStruct((3, dim, hidden), jnp.bfloat16),
        scalars=0,
        inputs=5,
        name="renew",
    )(grads, sent, one, three, two)

    result = jnp.zeros((rows, heads * dim), jnp.float32)
    for bits in order[::-1]:
        answer = whole_call(
            answer_kernel,
            jax.ShapeDtypeStruct((rows, dim), jnp.bfloat16),
            scalars=0,
            inputs=3,
            name="answer_%d" % bits,
        )(queries[bits], fresh, gain)
        if bits:
            answer = flip(answer, bits)
        source = head_of(seat ^ bits)
        result = lax.dynamic_update_slice(result, answer.astype(jnp.float32), (0, source * dim))
    return result


def one_head_each(mesh, heads, rows):
    count = mesh.shape["seq"]
    here = heads // mesh.shape["head"]
    fits = mesh.shape["head"] == 2 and count == 4 * len(PLANE) and count == 2 * here
    return fits and rows % (32 * count) == 0


def solution(mesh):
    in_specs = (
        P("seq", "head"),
        P("seq", "head"),
        P(None, "head"),
        P(None, "head"),
        P("head", None, None),
        P("head", None, None),
        P("head", None, None),
        P("head"),
    )
    out_specs = P("seq", "head")

    def layer(tokens, w_qkv, conv_w, prev_tail, w_one, *others):
        fits = one_head_each(mesh, w_one.shape[0], tokens.shape[0])
        mapped = jax.shard_map(
            head_device if fits else plain_device,
            mesh=mesh,
            in_specs=in_specs,
            out_specs=out_specs,
            check_vma=False,
        )
        return mapped(tokens, w_qkv, conv_w, prev_tail, w_one, *others)

    return layer
```
